128 devices in a mesh: group: 8 (over y_lo, x), mp: 16 (over y_hi, z, core).
Axes of the slice: x: 4, y: 4 (y_hi: 2, y_lo: 2; y = y_hi * 2 + y_lo), z: 4, core: 2. Of those that a mesh axis runs over, the one named last changes fastest.
Arguments:
- tokens: bfloat16 [640, 4096], P(None, 'group'), may hold values from -6 to 6
- trunk_gate: bfloat16 [4096, 11008], P('group', 'mp'), may hold values from -0.09375 to 0.09375
- trunk_up: bfloat16 [4096, 11008], P('group', 'mp'), may hold values from -0.09375 to 0.09375
- trunk_down: bfloat16 [11008, 4096], P('mp', 'group'), may hold values from -0.0546875 to 0.0546875
- head_gate: bfloat16 [8, 4096, 11008], P('group', None, 'mp'), may hold values from -0.09375 to 0.09375
- head_up: bfloat16 [8, 4096, 11008], P('group', None, 'mp'), may hold values from -0.09375 to 0.09375
- head_down: bfloat16 [8, 11008, 4096], P('group', 'mp'), may hold values from -0.0546875 to 0.0546875
- head_grads: bfloat16 [8, 640, 4096], P('group', None, 'mp'), may hold values from -6 to 6
Outputs:
- grad_x: bfloat16 [640, 4096], P('mp', 'group')
- grad_gate: float32 [4096, 11008], P('group', 'mp')
- grad_up: float32 [4096, 11008], P('group', 'mp')
- grad_down: float32 [11008, 4096], P('mp', 'group')
The draws below stay inside these ranges and needn't reach their ends.
All inputs are finite; a program needn't handle non-finite values.
Results may differ from the reference program's by a relative error of at most 0.009.
Values may be sent and summed in bfloat16 or wider, within the bound.
A program may use at most 128 MiB of HBM per device.

```python
import jax
import jax.numpy as jnp
from jax import lax

D = 4096
FF = 11008
TOKENS = 640
HEADS = 8


def levels(stream_key, shape, shards, smallest, largest):
    level, own = 1.0, jax.random.fold_in(stream_key, 6)
    for position, parts in shards:
        heights = jnp.exp(jax.random.uniform(jax.random.fold_in(own, position), (parts,), jnp.float32, smallest / len(shards), largest / len(shards)))
        level = level * jnp.repeat(heights, shape[position] // parts).reshape([-1 if axis == position else 1 for axis in range(len(shape))])
    return level


def scatter_about(rng, shape, spread, limit, shards=(), kind=jnp.bfloat16):
    level = levels(rng, shape, shards, -0.22, 0.18) if shards else 1.0
    drawn = jax.random.normal(rng, shape, jnp.float32) * spread * level
    return jnp.minimum(jnp.maximum(drawn, -limit), limit).astype(kind)


def setup_inputs(seed: int = 0) -> dict:
    key_list = jax.random.split(jax.random.key(seed), 9)
    tokens = scatter_about(key_list[0], (TOKENS, D), 1.0, 6.0, ((1, 8),))
    trunk_gate = scatter_about(key_list[1], (D, FF), D ** -0.5, 0.09375, ((0, 8), (1, 16)))
    trunk_up = scatter_about(key_list[2], (D, FF), D ** -0.5, 0.09375, ((0, 8), (1, 16)))
    trunk_down = scatter_about(key_list[3], (FF, D), FF ** -0.5, 0.0546875, ((0, 16), (1, 8)))
    head_gate = scatter_about(key_list[4], (HEADS, D, FF), D ** -0.5, 0.09375, ((0, 8), (2, 16)))
    head_up = scatter_about(key_list[5], (HEADS, D, FF), D ** -0.5, 0.09375, ((0, 8), (2, 16)))
    head_down = scatter_about(key_list[6], (HEADS, FF, D), FF ** -0.5, 0.0546875, ((0, 8), (1, 16)))
    head_grads = scatter_about(key_list[7], (HEADS, TOKENS, D), 1.0, 6.0, ((0, 8), (2, 16)))
    return {"tokens": tokens, "trunk_gate": trunk_gate, "trunk_up": trunk_up, "trunk_down": trunk_down, "head_gate": head_gate, "head_up": head_up, "head_down": head_down, "head_grads": head_grads}


def silu_grad(pre_act):
    sig = jax.nn.sigmoid(pre_act)
    return sig * (1.0 + pre_act * (1.0 - sig))

def contract_last(left, right):
    return lax.dot_general(left, right, (((1,), (1,)), ((), ())), preferred_element_type=jnp.float32)

def contract_first(left, right):
    return lax.dot_general(left, right, (((0,), (0,)), ((), ())), preferred_element_type=jnp.float32)

def reference(tokens, trunk_gate, trunk_up, trunk_down, head_gate, head_up, head_down, head_grads):
    gate_t = jnp.dot(tokens, trunk_gate, preferred_element_type=jnp.float32)
    up_t = jnp.dot(tokens, trunk_up, preferred_element_type=jnp.float32)
    hidden_t = (jax.nn.silu(gate_t) * up_t).astype(jnp.bfloat16)
    trunk_out = (tokens.astype(jnp.float32) + jnp.dot(hidden_t, trunk_down, preferred_element_type=jnp.float32)).astype(jnp.bfloat16)

    def one_head(running, head_item):
        gate_mat, up_mat, down_mat, cot_full = head_item
        head_pre = jnp.dot(trunk_out, gate_mat, preferred_element_type=jnp.float32)
        head_lin = jnp.dot(trunk_out, up_mat, preferred_element_type=jnp.float32)
        grad_hid = contract_last(cot_full, down_mat)
        gate_grad = (grad_hid * head_lin * silu_grad(head_pre)).astype(jnp.bfloat16)
        lin_grad = (grad_hid * jax.nn.silu(head_pre)).astype(jnp.bfloat16)
        term = cot_full.astype(jnp.float32) + contract_last(gate_grad, gate_mat) + contract_last(lin_grad, up_mat)
        return (running + term, None)
    start_sum = jnp.zeros((tokens.shape[0], tokens.shape[1]), jnp.float32)
    summed, _ = lax.scan(one_head, start_sum, (head_gate, head_up, head_down, head_grads))
    dtrunk = summed.astype(jnp.bfloat16)
    ghid_t = contract_last(dtrunk, trunk_down)
    dgate_t = (ghid_t * up_t * silu_grad(gate_t)).astype(jnp.bfloat16)
    dup_t = (ghid_t * jax.nn.silu(gate_t)).astype(jnp.bfloat16)
    grad_gate = contract_first(tokens, dgate_t)
    grad_up = contract_first(tokens, dup_t)
    grad_down = contract_first(hidden_t, dtrunk)
    grad_x = (dtrunk.astype(jnp.float32) + contract_last(dgate_t, trunk_gate) + contract_last(dup_t, trunk_up)).astype(jnp.bfloat16)
    return (grad_x, grad_gate, grad_up, grad_down)
```

```python
import functools

import jax
import jax.numpy as jnp
from jax import lax
from jax.experimental import pallas as pl
from jax.experimental.pallas import tpu as pltpu
from jax.sharding import PartitionSpec as P

F32 = jnp.float32
BF16 = jnp.bfloat16
MESH = pl.DeviceIdType.MESH
D = 4096
FL = 688
FP = 768
CW = 512
TILES = ((0, 256), (256, 256), (512, 176))
FINAL = (16, 16, 8)
ROWS = tuple(16 * f for f in FINAL)


def contract_first(left, right):
    return lax.dot_general(left, right, (((0,), (0,)), ((), ())), preferred_element_type=F32)


def dot(left, right):
    return jnp.dot(left, right, preferred_element_type=F32)


def dot_t(left, right):
    return lax.dot_general(left, right, (((1,), (1,)), ((), ())), preferred_element_type=F32)


def f32(x):
    return x.astype(F32)


def chunk_scratch(rows):
    r8, r4, r2, r16 = rows // 8, rows // 4, rows // 2, rows // 16
    shapes = dict(
        P=((8, 2, r8, FL), BF16),
        hid=((8, r8, FL), BF16),
        ab=((2, 8, r8, FL), BF16),
        D3=((rows, CW), BF16),
        D3r=((r2, CW), BF16),
        to=((rows, D), BF16),
        land=((rows, D), BF16),
        dk=((rows, 2 * FP), BF16),
        cr=((r2, D), BF16),
        E5=((r2, CW), BF16),
        dt=((rows, CW), BF16),
        G7=((8, r8, FL), BF16),
        gh=((8, r8, FL), BF16),
        dgu=((2, rows, FL), BF16),
        X9=((2, 2, 4, r16, CW), BF16),
        X9r=((2, 4, r16, CW), BF16),
        own=((r16, CW), BF16),
        c3=((7, r4, 128), BF16),
        e5=((7, r4, 128), BF16),
        c9=((7, r16, CW), BF16),
    )
    shapes["c7"] = ((7, r8, FL), BF16)
    for name, shape in (("c1", (2, r8, FL)), ("c5", (r2, CW))):
        shapes[name + "_rel"] = ((2, *shape), BF16)
        shapes[name + "_rl"] = ((2, *shape), BF16)
        shapes[name + "_rr"] = ((2, *shape), BF16)
        shapes[name + "_p"] = ((2, *shape), BF16)
    return shapes


SHARED = dict(
    W=((2 * FP, D), BF16),
    Wd=((FL, D), BF16),
    tg=((FL, CW), BF16),
    tu=((FL, CW), BF16),
    td=((FL, CW), BF16),
    hg=((sum(ROWS), 256), BF16),
    cot=((sum(ROWS), D), BF16),
    ghid=((sum(ROWS), FL), F32),
)
N_SEM = 420
ORDER = (
    "0c10102c10210120c1200211c2022102c10hh2021hh0hh10001001210110",
    "12010212012212012202122012120012102210210212102",
)


def layout():
    names, shapes = [], []
    for name, (shape, dtype) in SHARED.items():
        names.append(name)
        shapes.append(pltpu.VMEM(shape, dtype))
    for c, rows in enumerate(ROWS):
        names.append(f"tok{c}")
        shapes.append(pltpu.VMEM((rows, CW), BF16))
        for name, (shape, dtype) in chunk_scratch(rows).items():
            names.append(f"{name}{c}")
            shapes.append(pltpu.VMEM(shape, dtype))
    return names, shapes


class Net:
    def __init__(self, send_sem, recv_sem, copy_sem):
        self.send_sem, self.recv_sem, self.copy_sem = send_sem, recv_sem, copy_sem
        self.n = self.k = 0
        self.sent = []

    def send(self, src, dst, dev):
        copy = pltpu.make_async_remote_copy(
            src_ref=src,
            dst_ref=dst,
            send_sem=self.send_sem.at[self.n],
            recv_sem=self.recv_sem.at[self.n],
            device_id=dev,
            device_id_type=MESH,
        )
        self.n += 1
        copy.start()
        self.sent.append(copy)
        return copy

    def copy(self, src, dst):
        copy = pltpu.make_async_copy(src, dst, self.copy_sem.at[self.k])
        self.k += 1
        copy.start()
        return copy


def kernel(names, *refs):
    (tokens, tgate, tup, tdown, hgate, hup, hdown, hgrads, *rest) = refs
    outs, rest = rest[:4], rest[4:]
    S = dict(zip(names, rest[: len(names)], strict=True))
    net = Net(*rest[len(names) :])
    send = net.send

    g, m = lax.axis_index("group"), lax.axis_index("mp")
    yl, x = lax.div(g, 4), lax.rem(g, 4)
    yh, z, core = lax.div(m, 8), lax.rem(lax.div(m, 2), 4), lax.rem(m, 2)

    def ring(i, step):
        return lax.rem(i + step, 4)

    xr, xl = (yl * 4 + ring(x, 1), m), (yl * 4 + ring(x, 3), m)
    zr, zl = (g, yh * 8 + ring(z, 1) * 2 + core), (g, yh * 8 + ring(z, 3) * 2 + core)
    lp = ((1 - yl) * 4 + x, m)
    hp = (g, (1 - yh) * 8 + z * 2 + core)
    cp = (g, m + 1 - 2 * core)

    def across(dh, dx=0, dz=0):
        return (yl * 4 + ring(x, dx), lax.rem(yh + dh, 2) * 8 + ring(z, dz) * 2 + core)

    far_z = [(dh, dz, across(dh, dz=dz)) for dh in (0, 1) for dz in range(4) if dh or dz]
    far_x = [(dh, dx, across(dh, dx=dx)) for dh in (0, 1) for dx in range(4) if dh or dx]
    far_g = [
        (dh, dx, (lax.rem(yl + dh, 2) * 4 + ring(x, dx), m)) for dx in (1, 3, 2, 0) for dh in (0, 1) if dh or dx
    ]
    near = [dev for _, _, dev in far_g] + [zr, zl, hp, cp, across(0, dz=2)]
    near += [across(1, dx=i) for i in (1, 2, 3)] + [across(1, dz=i) for i in (1, 2, 3)]

    w_tok = [
        [
            net.copy(tokens.at[pl.ds(i * sum(FINAL) + sum(FINAL[:c]), f)], S[f"tok{c}"].at[pl.ds(i * f, f)])
            for i in range(16)
        ]
        for c, f in enumerate(FINAL)
    ]
    w_tg, w_tu = net.copy(tgate, S["tg"]), net.copy(tup, S["tu"])
    w_hg = [
        net.copy(
            hgrads.at[pl.ds(i * sum(FINAL) + sum(FINAL[:c]), f)], S["hg"].at[pl.ds(sum(ROWS[:c]) + i * f, f)]
        )
        for c, f in enumerate(FINAL)
        for i in range(16)
    ]
    w_td = net.copy(tdown, S["td"])
    w_hd = net.copy(hdown, S["Wd"])
    w_h = [
        net.copy(
            src.at[:, pl.ds((j * 4 + i) * 128, 128)],
            S["W"].at[pl.ds(top, FL), pl.ds((i * 8 + j % 4 * 2 + j // 4) * 128, 128)],
        )
        for src, top in ((hgate, 0), (hup, FP))
        for i in range(4)
        for j in range(8)
    ]
    for top in (FL, FP + FL):
        S["W"][top : top + FP - FL, :] = jnp.zeros((FP - FL, D), BF16)
    for c, rows in enumerate(ROWS):
        for last in (FP, 2 * FP):
            S[f"dk{c}"][:, last - 128 : last] = jnp.zeros((rows, 128), BF16)

    barrier = pltpu.get_barrier_semaphore()
    for dev in near:
        pl.semaphore_signal(barrier, inc=1, device_id=dev, device_id_type=MESH)

    def acc(dst, src):
        dst[...] = (f32(dst[...]) + f32(src[...])).astype(BF16)

    def rs_tail(win, bufs, r, devs, h, pdev, a, b, c1=None, d0=None, before_sum=None):
        rel, rl, rr, p = bufs
        rdev, ldev = devs
        yield
        a.wait_recv()
        acc(win(0, ring(r, 1)), rel.at[0])
        c0 = send(win(0, ring(r, 1)), rl.at[0], rdev)
        b.wait_recv()
        acc(win(1, ring(r, 3)), rel.at[1])
        d1 = send(win(1, ring(r, 3)), rr.at[1], ldev)
        if c1 is None:
            c1 = send(win(1, ring(r, 1)), rl.at[1], rdev)
            d0 = send(win(0, ring(r, 3)), rr.at[0], ldev)
        if before_sum is not None:
            before_sum()
        yield
        for copy in (c1, d0, c0, d1):
            copy.wait_recv()
        oh = 1 - h
        p[0] = (f32(win(oh, r)[...]) + f32(rl[oh]) + f32(rr[oh])).astype(BF16)
        q = send(p.at[0], p.at[1], pdev)
        yield
        q.wait_recv()
        return f32(win(h, r)[...]) + f32(rl[h]) + f32(rr[h]) + f32(p[1])

    def rs(win, bufs, r, devs, h, pdev):
        rel, rl, rr, _ = bufs
        rdev, ldev = devs
        a = send(win(0, ring(r, 2)), rel.at[0], rdev)
        b = send(win(1, ring(r, 2)), rel.at[1], ldev)
        return (yield from rs_tail(win, bufs, r, devs, h, pdev, a, b))

    def ag(win, r, devs, h, pdev, have=lambda h, r: None):
        rdev, ldev = devs
        R, L, O = ring(r, 1), ring(r, 3), ring(r, 2)

        def go(h, r, dev):
            return send(win(h, r), win(h, r), dev)

        p, a1, b1 = go(h, r, pdev), go(h, r, rdev), go(h, r, ldev)
        have(h, r)
        yield
        p.wait_recv()
        a2, b2 = go(1 - h, r, rdev), go(1 - h, r, ldev)
        have(1 - h, r)
        yield
        a1.wait_recv()
        b1.wait_recv()
        have(h, L)
        have(h, R)
        a2.wait_recv()
        fr = go(0, L, rdev)
        b2.wait_recv()
        fl = go(1, R, ldev)
        have(1 - h, L)
        have(1 - h, R)
        yield
        fr.wait_recv()
        fl.wait_recv()
        have(0, O)
        have(1, O)

    cot_sent = []

    def rs_far(win, buf, h, r, far):
        copies = [send(win(lax.rem(h + dh, 2), ring(r, dr)), buf.at[i], dev) for i, (dh, dr, dev) in enumerate(far)]
        yield
        total = f32(win(h, r)[...])
        for i, copy in enumerate(copies):
            copy.wait_recv()
            total += f32(buf[i])
        return total

    def ag_far(win, h, r, far):
        copies = [send(win(h, r), win(h, r), dev) for _, _, dev in far]
        yield
        for copy in copies:
            copy.wait_recv()

    def gather_cot():
        cot, half = S["cot"], sum(ROWS) // 2

        def win(h, zz, cc=core, rows=None):
            cols = pl.ds(pl.multiple_of((h * 8 + zz * 2 + cc) * 256, 256), 256)
            return cot.at[:, cols] if rows is None else cot.at[pl.ds(rows, half), cols]

        to_core = []

        def go(src, dst, dev):
            copy = send(src, dst, dev)
            cot_sent.append(net.sent.pop())
            return copy

        def have(h, zz):
            to_core.append(go(win(h, zz), win(h, zz), cp))

        def both(h, zz, dev):
            return go(win(h, zz), win(h, zz), dev)

        mine = win(yh, z)
        for copy in w_hg:
            copy.wait()
        keep = net.copy(S["hg"], mine)
        p, a1, b1, k = (go(S["hg"], mine, dev) for dev in (hp, zr, zl, cp))
        to_core.append(k)
        yield
        p.wait_recv()
        a2, b2 = both(1 - yh, z, zr), both(1 - yh, z, zl)
        have(1 - yh, z)
        keep.wait()
        yield
        a1.wait_recv()
        b1.wait_recv()
        L, R, O = ring(z, 3), ring(z, 1), ring(z, 2)
        f1 = go(win(yh, L, rows=0), win(yh, L, rows=0), zr)
        e1 = go(win(yh, R, rows=half), win(yh, R, rows=half), zl)
        have(yh, L)
        have(yh, R)
        yield
        a2.wait_recv()
        b2.wait_recv()
        f2 = go(win(1 - yh, L, rows=0), win(1 - yh, L, rows=0), zr)
        e2 = go(win(1 - yh, R, rows=half), win(1 - yh, R, rows=half), zl)
        have(1 - yh, L)
        have(1 - yh, R)
        yield
        f1.wait_recv()
        e1.wait_recv()
        have(yh, O)
        f2.wait_recv()
        e2.wait_recv()
        have(1 - yh, O)
        for copy in to_core:
            copy.wait_recv()

    def head_hidden():
        w_hd.wait()
        row = 0
        for rows in ROWS:
            for n, w in ((0, 512), (512, 176)):
                S["ghid"][row : row + rows, n : n + w] = dot_t(S["cot"][row : row + rows, :], S["Wd"][n : n + w, :])
                yield
            row += rows

    reached = set()

    def once(key, copies=()):
        if key in reached:
            return False
        reached.add(key)
        for copy in copies:
            copy.wait()
        return True

    def chunk(c):
        rows = ROWS[c]
        row0 = sum(ROWS[:c])
        r8, r4, r2, r16 = rows // 8, rows // 4, rows // 2, rows // 16
        B = {n[:-1]: r for n, r in S.items() if n.endswith(str(c))}
        bufs = {n: tuple(B[n + e] for e in ("_rel", "_rl", "_rr", "_p")) for n in ("c1", "c5")}
        xdev, zdev = (xr, xl), (zr, zl)
        on_z = c != 1
        if on_z:
            small, far_small, big, big_dev = x, far_x, z, zdev
        else:
            small, far_small, big, big_dev = z, far_z, x, xdev

        def half(cc):
            return pl.ds(pl.multiple_of(cc * r2, r2), r2)

        def quarter(cc, h):
            return pl.ds(pl.multiple_of(cc * r2 + h * r4, r4), r4)

        def cols(i, w):
            return pl.ds(pl.multiple_of(i * w, w), w)

        for copy in w_tok[c]:
            copy.wait()
        once("gate", [w_tg, w_tu])
        for i, w_ref in enumerate((S["tg"], S["tu"])):
            for n, w in TILES:
                part = dot_t(B["tok"][...], w_ref[n : n + w, :])
                for j in range(8):
                    B["P"][j, i, :, n : n + w] = part[j * r8 : (j + 1) * r8].astype(BF16)
        yield
        total = yield from rs(lambda h, r: B["P"].at[h * 4 + r], bufs["c1"], x, xdev, yl, lp)
        hid, ab = B["hid"], B["ab"]
        gate, up = total[0], total[1]
        sig = jax.nn.sigmoid(gate)
        hid[g] = (gate * sig * up).astype(BF16)
        factors = ag(lambda h, r: ab.at[:, h * 4 + r], x, xdev, yl, lp)
        ab[0, g] = (up * (sig * (1.0 + gate * (1.0 - sig)))).astype(BF16)
        ab[1, g] = (gate * sig).astype(BF16)
        yield from ag(lambda h, r: hid.at[h * 4 + r], x, xdev, yl, lp)
        once("down", [w_td])
        B["D3"][...] = dot(hid[...].reshape(rows, FL), S["td"][...]).astype(BF16)
        k = send(B["D3"].at[half(1 - core)], B["D3r"], cp)
        next(factors)
        yield
        k.wait_recv()
        acc(B["D3"].at[half(core)], B["D3r"])
        total = yield from rs_far(lambda h, r: B["D3"].at[quarter(core, h), cols(r, 128)], B["c3"], yh, z, far_z)
        to = B["to"]
        land = B["land"]
        own = f32(B["tok"][quarter(core, yh), cols(z, 128)])

        def small_win(h, r):
            block = z * 8 + yl * 4 + r if on_z else (yl * 4 + x) * 4 + r
            return land.at[quarter(core, h), cols(block, 128)]

        def big_win(h, r):
            return land.at[half(core), cols(r * 2 + h if on_z else h * 4 + r, 512)]

        small_win(yh, small)[...] = (own + total).astype(BF16)
        yield from ag_far(small_win, yh, small, far_small)
        to_core = []

        def have(h, r):
            to_core.append(send(big_win(h, r), big_win(h, r), cp))

        yield from ag(big_win, big, big_dev, yl, lp, have)
        next(factors)
        yield
        for copy in to_core:
            copy.wait_recv()
        for zz in range(4):
            for g_x in range(4):
                for g_y in range(2):
                    i = zz * 8 + g_x * 2 + g_y
                    j = zz * 8 + g_y * 4 + g_x if on_z else (g_y * 4 + g_x) * 4 + zz
                    to[:, i * 128 : i * 128 + 128] = land[:, j * 128 : j * 128 + 128]
        next(factors)
        yield "in"
        once("head", w_h)
        for n, w in TILES:
            pair = dot_t(to[...], jnp.concatenate([S["W"][n : n + 256, :], S["W"][FP + n : FP + n + 256, :]]))
            pre, lin = pair[:, :w], pair[:, 256 : 256 + w]
            grad = S["ghid"][row0 : row0 + rows, n : n + w]
            sig = jax.nn.sigmoid(pre)
            B["dk"][:, n : n + w] = (grad * lin * (sig * (1.0 + pre * (1.0 - sig)))).astype(BF16)
            B["dk"][:, FP + n : FP + n + w] = (grad * (pre * sig)).astype(BF16)
            yield "tile"
        for _ in factors:
            pass
        dp = S["cot"]
        while cot_sent:
            cot_sent.pop().wait_send()

        def dhalf(cc):
            return pl.ds(pl.multiple_of(row0 + cc * r2, 64), r2)

        order = (ring(big, 2), ring(big, 1), ring(big, 3), big)
        ks = []

        def dcols(r, h):
            return cols(r * 2 + h if on_z else h * 4 + r, 512)

        def dwin(h, r):
            return dp.at[dhalf(core), dcols(r, h)]

        def finish(i):
            for h in range(2):
                ks[i][h].wait_recv()
                acc(dwin(h, order[i]), B["cr"].at[:, dcols(order[i], h)])

        rel, rl, rr, _ = bufs["c5"]
        g_own, z_own = lax.div(m, 2), lax.rem(m, 2) * 2
        for i, rb in enumerate(order):
            if on_z:

                @pl.loop(0, 2)
                def _(t):
                    part = dot(B["dk"][...], S["W"][:, pl.ds(pl.multiple_of(rb * 1024 + t * 512, 512), 512)])
                    for q in range(4):
                        w = pl.ds(pl.multiple_of(rb * 1024 + q % 2 * 512 + (t * 2 + q // 2) * 128, 128), 128)
                        dp[row0 : row0 + rows, w] = part[:, q * 128 : q * 128 + 128].astype(BF16)

            else:

                @pl.loop(0, 2)
                def _(t):
                    weights = [
                        S["W"][:, pl.ds(pl.multiple_of((t * 2 + j) * 1024 + rb * 256, 256), 256)] for j in range(2)
                    ]
                    part = dot(B["dk"][...], jnp.concatenate(weights, axis=1))
                    for q in range(4):
                        w = pl.ds(pl.multiple_of((q % 2 * 4 + rb) * 512 + (t * 2 + q // 2) * 128, 128), 128)
                        dp[row0 : row0 + rows, w] = part[:, q * 128 : q * 128 + 128].astype(BF16)

            for t in range(2):
                mine = z_own + t == rb if on_z else lax.rem(g_own, 4) == rb

                @pl.when(mine)
                def _():
                    w = cols((z_own + t) * 8 + g_own if on_z else g_own * 4 + z_own + t, 128)
                    dp[row0 : row0 + rows, w] = (
                        f32(dp[row0 : row0 + rows, w]) + f32(S["hg"][row0 : row0 + rows, t * 128 : t * 128 + 128])
                    ).astype(BF16)

            ks.append(
                [send(dp.at[dhalf(1 - core), dcols(rb, h)], B["cr"].at[:, dcols(rb, h)], cp) for h in range(2)]
            )
            yield "back"
            if i == 1:
                finish(0)
                a = send(dwin(0, order[0]), rel.at[0], big_dev[0])
                b = send(dwin(1, order[0]), rel.at[1], big_dev[1])
            if i == 2:
                finish(1)
                c1 = send(dwin(1, order[1]), rl.at[1], big_dev[0])
            if i == 3:
                finish(2)
                d0 = send(dwin(0, order[2]), rr.at[0], big_dev[1])
        total = yield from rs_tail(dwin, bufs["c5"], big, big_dev, yl, lp, a, b, c1, d0, lambda: finish(3))
        B["E5"][...] = total.astype(BF16)
        total = yield from rs_far(
            lambda h, r: B["E5"].at[pl.ds(pl.multiple_of(h * r4, r4), r4), cols(r, 128)], B["e5"], yh, small, far_small
        )
        dt = B["dt"]
        dt[quarter(core, yh), cols(z, 128)] = total.astype(BF16)
        yield from ag_far(lambda h, r: dt.at[quarter(core, h), cols(r, 128)], yh, z, far_z)
        k = send(dt.at[half(core)], dt.at[half(core)], cp)
        yield
        k.wait_recv()
        keep = net.copy(dt.at[pl.ds(m * r16, r16)], B["own"])
        for n, w in TILES:
            part = dot_t(dt[...], S["td"][n : n + w, :])
            for j in range(8):
                B["G7"][j, :, n : n + w] = part[j * r8 : (j + 1) * r8].astype(BF16)
        more = rs_far(lambda h, r: B["G7"].at[h * 4 + r], B["c7"], yl, x, far_g)
        next(more)

        def gather_rows(out, left, right):
            first = once(out)
            for n, w in TILES:
                part = contract_first(left[:, n : n + w], right)
                if first:
                    outs[out][n : n + w, :] = part
                else:
                    outs[out][n : n + w, :] += part

        gather_rows(3, hid[...].reshape(rows, FL), dt[...])
        yield
        total = yield from more
        gh, dgu = B["gh"], B["dgu"]
        gh[g] = total.astype(BF16)
        yield from ag_far(lambda h, r: gh.at[h * 4 + r], yl, x, far_g)
        for i in range(2):
            dgu[i] = (f32(gh[...]) * f32(ab[i])).astype(BF16).reshape(rows, FL)
        part = dot(dgu[0], S["tg"][...]) + dot(dgu[1], S["tu"][...])
        X9 = B["X9"]
        for i in range(16):
            X9[i % 2, i // 8, i // 2 % 4] = part[i * r16 : (i + 1) * r16].astype(BF16)
        k = send(X9.at[1 - core], B["X9r"], cp)
        gather_rows(1, dgu[0], B["tok"][...])
        yield
        k.wait_recv()
        acc(X9.at[core], B["X9r"])
        more = rs_far(lambda h, r: X9.at[core, h, r], B["c9"], yh, z, far_z)
        next(more)
        gather_rows(2, dgu[1], B["tok"][...])
        yield
        total = yield from more
        keep.wait()
        outs[0][sum(FINAL[:c]) : sum(FINAL[: c + 1]), :] = (f32(B["own"][...]) + total).astype(BF16)

    gens = {"c": gather_cot(), "h": head_hidden()} | {str(c): chunk(c) for c in range(len(ROWS))}

    def step(gen):
        return next(gen, "end")

    for c in range(len(ROWS)):
        step(gens[str(c)])
    pl.semaphore_wait(barrier, len(near))
    for name in "".join(ORDER):
        step(gens[name])
    for gen in gens.values():
        while step(gen) != "end":
            pass
    for copy in net.sent:
        copy.wait_send()


def body(tokens, trunk_gate, trunk_up, trunk_down, head_gate, head_up, head_down, head_grads):
    names, shapes = layout()
    grad_x, grad_gate, grad_up, grad_down = pl.pallas_call(
        functools.partial(kernel, names),
        out_shape=[
            pltpu.VMEM((sum(FINAL), CW), BF16),
            pltpu.VMEM((FL, CW), F32),
            pltpu.VMEM((FL, CW), F32),
            pltpu.VMEM((FL, CW), F32),
        ],
        in_specs=[pl.BlockSpec(memory_space=pl.ANY)] * 8,
        out_specs=[pl.BlockSpec(memory_space=pltpu.VMEM)] * 4,
        scratch_shapes=[
            *shapes,
            pltpu.SemaphoreType.DMA((N_SEM,)),
            pltpu.SemaphoreType.DMA((N_SEM,)),
            pltpu.SemaphoreType.DMA((220,)),
        ],
        compiler_params=pltpu.CompilerParams(
            collective_id=0, has_side_effects=True, vmem_limit_bytes=62500000
        ),
    )(
        tokens,
        trunk_gate.T,
        trunk_up.T,
        trunk_down,
        head_gate[0].T,
        head_up[0].T,
        head_down[0],
        head_grads[0],
    )
    return grad_x, grad_gate.T, grad_up.T, grad_down


def solution(mesh):
    return jax.shard_map(
        body,
        mesh=mesh,
        in_specs=(
            P(None, "group"),
            P("group", "mp"),
            P("group", "mp"),
            P("mp", "group"),
            P("group", None, "mp"),
            P("group", None, "mp"),
            P("group", "mp", None),
            P("group", None, "mp"),
        ),
        out_specs=(P("mp", "group"), P("group", "mp"), P("group", "mp"), P("mp", "group")),
        check_vma=False,
    )
```

```python
import functools

import jax
import jax.numpy as jnp
from jax import lax
from jax.experimental import pallas as pl
from jax.experimental.pallas import tpu as pltpu
from jax.sharding import PartitionSpec as P

F32 = jnp.float32
BF16 = jnp.bfloat16
MESH = pl.DeviceIdType.MESH
D = 4096
FL = 688
FP = 768
CW = 512
TILES = ((0, 256), (256, 256), (512, 176))
FINAL = (16, 16, 8)
ROWS = tuple(16 * f for f in FINAL)


def contract_first(left, right):
    return lax.dot_general(left, right, (((0,), (0,)), ((), ())), preferred_element_type=F32)


def dot(left, right):
    return jnp.dot(left, right, preferred_element_type=F32)


def dot_t(left, right):
    return lax.dot_general(left, right, (((1,), (1,)), ((), ())), preferred_element_type=F32)


def f32(x):
    return x.astype(F32)


def chunk_scratch(rows):
    r8, r4, r2, r16 = rows // 8, rows // 4, rows // 2, rows // 16
    shapes = dict(
        P=((8, 2, r8, FL), BF16),
        hid=((8, r8, FL), BF16),
        ab=((2, 8, r8, FL), BF16),
        D3=((rows, CW), BF16),
        D3r=((r2, CW), BF16),
        to=((rows, D), BF16),
        land=((rows, D), BF16),
        dk=((rows, 2 * FP), BF16),
        cr=((r2, D), BF16),
        E5=((r2, CW), BF16),
        dt=((rows, CW), BF16),
        G7=((8, r8, FL), BF16),
        gh=((8, r8, FL), BF16),
        dgu=((2, rows, FL), BF16),
        X9=((2, 2, 4, r16, CW), BF16),
        X9r=((2, 4, r16, CW), BF16),
        own=((r16, CW), BF16),
        c3=((7, r4, 128), BF16),
        e5=((7, r4, 128), BF16),
        c9=((7, r16, CW), BF16),
    )
    shapes["c7"] = ((7, r8, FL), BF16)
    for name, shape in (("c1", (2, r8, FL)), ("c5", (r2, CW))):
        shapes[name + "_rel"] = ((2, *shape), BF16)
        shapes[name + "_rl"] = ((2, *shape), BF16)
        shapes[name + "_rr"] = ((2, *shape), BF16)
        shapes[name + "_p"] = ((2, *shape), BF16)
    return shapes


SHARED = dict(
    W=((2 * FP, D), BF16),
    Wd=((FL, D), BF16),
    tg=((FL, CW), BF16),
    tu=((FL, CW), BF16),
    td=((FL, CW), BF16),
    hg=((sum(ROWS), 256), BF16),
    cot=((sum(ROWS), D), BF16),
    ghid=((sum(ROWS), FL), F32),
)
N_SEM = 420
ORDER = (
    "0c10102c10210120c1200211c2022102c10h2021h0h10001001210110120",
    "10212012212012202122012120012102210210212102",
)


def layout():
    names, shapes = [], []
    for name, (shape, dtype) in SHARED.items():
        names.append(name)
        shapes.append(pltpu.VMEM(shape, dtype))
    for c, rows in enumerate(ROWS):
        names.append(f"tok{c}")
        shapes.append(pltpu.VMEM((rows, CW), BF16))
        for name, (shape, dtype) in chunk_scratch(rows).items():
            names.append(f"{name}{c}")
            shapes.append(pltpu.VMEM(shape, dtype))
    return names, shapes


class Net:
    def __init__(self, send_sem, recv_sem, copy_sem):
        self.send_sem, self.recv_sem, self.copy_sem = send_sem, recv_sem, copy_sem
        self.n = self.k = 0
        self.sent = []

    def send(self, src, dst, dev):
        copy = pltpu.make_async_remote_copy(
            src_ref=src,
            dst_ref=dst,
            send_sem=self.send_sem.at[self.n],
            recv_sem=self.recv_sem.at[self.n],
            device_id=dev,
            device_id_type=MESH,
        )
        self.n += 1
        copy.start()
        self.sent.append(copy)
        return copy

    def copy(self, src, dst):
        copy = pltpu.make_async_copy(src, dst, self.copy_sem.at[self.k])
        self.k += 1
        copy.start()
        return copy


def kernel(names, *refs):
    (tokens, tgate, tup, tdown, hgate, hup, hdown, hgrads, *rest) = refs
    outs, rest = rest[:4], rest[4:]
    S = dict(zip(names, rest[: len(names)], strict=True))
    net = Net(*rest[len(names) :])
    send = net.send

    g, m = lax.axis_index("group"), lax.axis_index("mp")
    yl, x = lax.div(g, 4), lax.rem(g, 4)
    yh, z, core = lax.div(m, 8), lax.rem(lax.div(m, 2), 4), lax.rem(m, 2)

    def ring(i, step):
        return lax.rem(i + step, 4)

    xr, xl = (yl * 4 + ring(x, 1), m), (yl * 4 + ring(x, 3), m)
    zr, zl = (g, yh * 8 + ring(z, 1) * 2 + core), (g, yh * 8 + ring(z, 3) * 2 + core)
    lp = ((1 - yl) * 4 + x, m)
    hp = (g, (1 - yh) * 8 + z * 2 + core)
    cp = (g, m + 1 - 2 * core)

    def across(dh, dx=0, dz=0):
        return (yl * 4 + ring(x, dx), lax.rem(yh + dh, 2) * 8 + ring(z, dz) * 2 + core)

    far_z = [(dh, dz, across(dh, dz=dz)) for dh in (0, 1) for dz in range(4) if dh or dz]
    far_x = [(dh, dx, across(dh, dx=dx)) for dh in (0, 1) for dx in range(4) if dh or dx]
    far_g = [
        (dh, dx, (lax.rem(yl + dh, 2) * 4 + ring(x, dx), m)) for dx in (1, 3, 2, 0) for dh in (0, 1) if dh or dx
    ]
    near = [dev for _, _, dev in far_g] + [zr, zl, hp, cp, across(0, dz=2)]
    near += [across(1, dx=i) for i in (1, 2, 3)] + [across(1, dz=i) for i in (1, 2, 3)]

    w_tok = [
        [
            net.copy(tokens.at[pl.ds(i * sum(FINAL) + sum(FINAL[:c]), f)], S[f"tok{c}"].at[pl.ds(i * f, f)])
            for i in range(16)
        ]
        for c, f in enumerate(FINAL)
    ]
    w_tg, w_tu = net.copy(tgate, S["tg"]), net.copy(tup, S["tu"])
    w_hg = [
        net.copy(
            hgrads.at[pl.ds(i * sum(FINAL) + sum(FINAL[:c]), f)], S["hg"].at[pl.ds(sum(ROWS[:c]) + i * f, f)]
        )
        for c, f in enumerate(FINAL)
        for i in range(16)
    ]
    w_td = net.copy(tdown, S["td"])
    w_hd = net.copy(hdown, S["Wd"])
    w_h = [
        net.copy(
            src.at[:, pl.ds((j * 4 + i) * 128, 128)],
            S["W"].at[pl.ds(top, FL), pl.ds((i * 8 + j % 4 * 2 + j // 4) * 128, 128)],
        )
        for src, top in ((hgate, 0), (hup, FP))
        for i in range(4)
        for j in range(8)
    ]
    for top in (FL, FP + FL):
        S["W"][top : top + FP - FL, :] = jnp.zeros((FP - FL, D), BF16)
    for c, rows in enumerate(ROWS):
        for last in (FP, 2 * FP):
            S[f"dk{c}"][:, last - 128 : last] = jnp.zeros((rows, 128), BF16)

    barrier = pltpu.get_barrier_semaphore()
    for dev in near:
        pl.semaphore_signal(barrier, inc=1, device_id=dev, device_id_type=MESH)

    def acc(dst, src):
        dst[...] = (f32(dst[...]) + f32(src[...])).astype(BF16)

    def rs_tail(win, bufs, r, devs, h, pdev, a, b, c1=None, d0=None, before_sum=None):
        rel, rl, rr, p = bufs
        rdev, ldev = devs
        yield
        a.wait_recv()
        acc(win(0, ring(r, 1)), rel.at[0])
        c0 = send(win(0, ring(r, 1)), rl.at[0], rdev)
        b.wait_recv()
        acc(win(1, ring(r, 3)), rel.at[1])
        d1 = send(win(1, ring(r, 3)), rr.at[1], ldev)
        if c1 is None:
            c1 = send(win(1, ring(r, 1)), rl.at[1], rdev)
            d0 = send(win(0, ring(r, 3)), rr.at[0], ldev)
        if before_sum is not None:
            before_sum()
        yield
        for copy in (c1, d0, c0, d1):
            copy.wait_recv()
        oh = 1 - h
        p[0] = (f32(win(oh, r)[...]) + f32(rl[oh]) + f32(rr[oh])).astype(BF16)
        q = send(p.at[0], p.at[1], pdev)
        yield
        q.wait_recv()
        return f32(win(h, r)[...]) + f32(rl[h]) + f32(rr[h]) + f32(p[1])

    def rs(win, bufs, r, devs, h, pdev):
        rel, rl, rr, _ = bufs
        rdev, ldev = devs
        a = send(win(0, ring(r, 2)), rel.at[0], rdev)
        b = send(win(1, ring(r, 2)), rel.at[1], ldev)
        return (yield from rs_tail(win, bufs, r, devs, h, pdev, a, b))

    def ag(win, r, devs, h, pdev, have=lambda h, r: None):
        rdev, ldev = devs
        R, L, O = ring(r, 1), ring(r, 3), ring(r, 2)

        def go(h, r, dev):
            return send(win(h, r), win(h, r), dev)

        p, a1, b1 = go(h, r, pdev), go(h, r, rdev), go(h, r, ldev)
        have(h, r)
        yield
        p.wait_recv()
        a2, b2 = go(1 - h, r, rdev), go(1 - h, r, ldev)
        have(1 - h, r)
        yield
        a1.wait_recv()
        b1.wait_recv()
        have(h, L)
        have(h, R)
        a2.wait_recv()
        fr = go(0, L, rdev)
        b2.wait_recv()
        fl = go(1, R, ldev)
        have(1 - h, L)
        have(1 - h, R)
        yield
        fr.wait_recv()
        fl.wait_recv()
        have(0, O)
        have(1, O)

    cot_sent = []

    def rs_far(win, buf, h, r, far):
        copies = [send(win(lax.rem(h + dh, 2), ring(r, dr)), buf.at[i], dev) for i, (dh, dr, dev) in enumerate(far)]
        yield
        total = f32(win(h, r)[...])
        for i, copy in enumerate(copies):
            copy.wait_recv()
            total += f32(buf[i])
        return total

    def ag_far(win, h, r, far):
        copies = [send(win(h, r), win(h, r), dev) for _, _, dev in far]
        yield
        for copy in copies:
            copy.wait_recv()

    def gather_cot():
        cot, half = S["cot"], sum(ROWS) // 2

        def win(h, zz, cc=core, rows=None):
            cols = pl.ds(pl.multiple_of((h * 8 + zz * 2 + cc) * 256, 256), 256)
            return cot.at[:, cols] if rows is None else cot.at[pl.ds(rows, half), cols]

        to_core = []

        def go(src, dst, dev):
            copy = send(src, dst, dev)
            cot_sent.append(net.sent.pop())
            return copy

        def have(h, zz):
            to_core.append(go(win(h, zz), win(h, zz), cp))

        def both(h, zz, dev):
            return go(win(h, zz), win(h, zz), dev)

        mine = win(yh, z)
        for copy in w_hg:
            copy.wait()
        keep = net.copy(S["hg"], mine)
        p, a1, b1, k = (go(S["hg"], mine, dev) for dev in (hp, zr, zl, cp))
        to_core.append(k)
        yield
        p.wait_recv()
        a2, b2 = both(1 - yh, z, zr), both(1 - yh, z, zl)
        have(1 - yh, z)
        keep.wait()
        yield
        a1.wait_recv()
        b1.wait_recv()
        L, R, O = ring(z, 3), ring(z, 1), ring(z, 2)
        f1 = go(win(yh, L, rows=0), win(yh, L, rows=0), zr)
        e1 = go(win(yh, R, rows=half), win(yh, R, rows=half), zl)
        have(yh, L)
        have(yh, R)
        yield
        a2.wait_recv()
        b2.wait_recv()
        f2 = go(win(1 - yh, L, rows=0), win(1 - yh, L, rows=0), zr)
        e2 = go(win(1 - yh, R, rows=half), win(1 - yh, R, rows=half), zl)
        have(1 - yh, L)
        have(1 - yh, R)
        yield
        f1.wait_recv()
        e1.wait_recv()
        have(yh, O)
        f2.wait_recv()
        e2.wait_recv()
        have(1 - yh, O)
        for copy in to_core:
            copy.wait_recv()

    def head_hidden():
        w_hd.wait()
        for n, w in TILES:
            for row in (0, 320):
                S["ghid"][row : row + 320, n : n + w] = dot_t(S["cot"][row : row + 320, :], S["Wd"][n : n + w, :])
            yield

    reached = set()

    def once(key, copies=()):
        if key in reached:
            return False
        reached.add(key)
        for copy in copies:
            copy.wait()
        return True

    def chunk(c):
        rows = ROWS[c]
        row0 = sum(ROWS[:c])
        r8, r4, r2, r16 = rows // 8, rows // 4, rows // 2, rows // 16
        B = {n[:-1]: r for n, r in S.items() if n.endswith(str(c))}
        bufs = {n: tuple(B[n + e] for e in ("_rel", "_rl", "_rr", "_p")) for n in ("c1", "c5")}
        xdev, zdev = (xr, xl), (zr, zl)
        on_z = c != 1
        if on_z:
            small, far_small, big, big_dev = x, far_x, z, zdev
        else:
            small, far_small, big, big_dev = z, far_z, x, xdev

        def half(cc):
            return pl.ds(pl.multiple_of(cc * r2, r2), r2)

        def quarter(cc, h):
            return pl.ds(pl.multiple_of(cc * r2 + h * r4, r4), r4)

        def cols(i, w):
            return pl.ds(pl.multiple_of(i * w, w), w)

        for copy in w_tok[c]:
            copy.wait()
        once("gate", [w_tg, w_tu])
        for i, w_ref in enumerate((S["tg"], S["tu"])):
            for n, w in TILES:
                part = dot_t(B["tok"][...], w_ref[n : n + w, :])
                for j in range(8):
                    B["P"][j, i, :, n : n + w] = part[j * r8 : (j + 1) * r8].astype(BF16)
        yield
        total = yield from rs(lambda h, r: B["P"].at[h * 4 + r], bufs["c1"], x, xdev, yl, lp)
        hid, ab = B["hid"], B["ab"]
        gate, up = total[0], total[1]
        sig = jax.nn.sigmoid(gate)
        hid[g] = (gate * sig * up).astype(BF16)
        factors = ag(lambda h, r: ab.at[:, h * 4 + r], x, xdev, yl, lp)
        ab[0, g] = (up * (sig * (1.0 + gate * (1.0 - sig)))).astype(BF16)
        ab[1, g] = (gate * sig).astype(BF16)
        yield from ag(lambda h, r: hid.at[h * 4 + r], x, xdev, yl, lp)
        once("down", [w_td])
        B["D3"][...] = dot(hid[...].reshape(rows, FL), S["td"][...]).astype(BF16)
        k = send(B["D3"].at[half(1 - core)], B["D3r"], cp)
        next(factors)
        yield
        k.wait_recv()
        acc(B["D3"].at[half(core)], B["D3r"])
        total = yield from rs_far(lambda h, r: B["D3"].at[quarter(core, h), cols(r, 128)], B["c3"], yh, z, far_z)
        to = B["to"]
        land = B["land"]
        own = f32(B["tok"][quarter(core, yh), cols(z, 128)])

        def small_win(h, r):
            block = z * 8 + yl * 4 + r if on_z else (yl * 4 + x) * 4 + r
            return land.at[quarter(core, h), cols(block, 128)]

        def big_win(h, r):
            return land.at[half(core), cols(r * 2 + h if on_z else h * 4 + r, 512)]

        small_win(yh, small)[...] = (own + total).astype(BF16)
        yield from ag_far(small_win, yh, small, far_small)
        to_core = []

        def have(h, r):
            to_core.append(send(big_win(h, r), big_win(h, r), cp))

        yield from ag(big_win, big, big_dev, yl, lp, have)
        next(factors)
        yield
        for copy in to_core:
            copy.wait_recv()
        for zz in range(4):
            for g_x in range(4):
                for g_y in range(2):
                    i = zz * 8 + g_x * 2 + g_y
                    j = zz * 8 + g_y * 4 + g_x if on_z else (g_y * 4 + g_x) * 4 + zz
                    to[:, i * 128 : i * 128 + 128] = land[:, j * 128 : j * 128 + 128]
        next(factors)
        yield "in"
        once("head", w_h)
        for n, w in TILES:
            pair = dot_t(to[...], jnp.concatenate([S["W"][n : n + 256, :], S["W"][FP + n : FP + n + 256, :]]))
            pre, lin = pair[:, :w], pair[:, 256 : 256 + w]
            grad = S["ghid"][row0 : row0 + rows, n : n + w]
            sig = jax.nn.sigmoid(pre)
            B["dk"][:, n : n + w] = (grad * lin * (sig * (1.0 + pre * (1.0 - sig)))).astype(BF16)
            B["dk"][:, FP + n : FP + n + w] = (grad * (pre * sig)).astype(BF16)
            yield "tile"
        for _ in factors:
            pass
        dp = S["cot"]
        while cot_sent:
            cot_sent.pop().wait_send()

        def dhalf(cc):
            return pl.ds(pl.multiple_of(row0 + cc * r2, 64), r2)

        order = (ring(big, 2), ring(big, 1), ring(big, 3), big)
        ks = []

        def dcols(r, h):
            return cols(r * 2 + h if on_z else h * 4 + r, 512)

        def dwin(h, r):
            return dp.at[dhalf(core), dcols(r, h)]

        def finish(i):
            for h in range(2):
                ks[i][h].wait_recv()
                acc(dwin(h, order[i]), B["cr"].at[:, dcols(order[i], h)])

        rel, rl, rr, _ = bufs["c5"]
        g_own, z_own = lax.div(m, 2), lax.rem(m, 2) * 2
        for i, rb in enumerate(order):
            if on_z:

                @pl.loop(0, 2)
                def _(t):
                    part = dot(B["dk"][...], S["W"][:, pl.ds(pl.multiple_of(rb * 1024 + t * 512, 512), 512)])
                    for q in range(4):
                        w = pl.ds(pl.multiple_of(rb * 1024 + q % 2 * 512 + (t * 2 + q // 2) * 128, 128), 128)
                        dp[row0 : row0 + rows, w] = part[:, q * 128 : q * 128 + 128].astype(BF16)

            else:

                @pl.loop(0, 2)
                def _(t):
                    weights = [
                        S["W"][:, pl.ds(pl.multiple_of((t * 2 + j) * 1024 + rb * 256, 256), 256)] for j in range(2)
                    ]
                    part = dot(B["dk"][...], jnp.concatenate(weights, axis=1))
                    for q in range(4):
                        w = pl.ds(pl.multiple_of((q % 2 * 4 + rb) * 512 + (t * 2 + q // 2) * 128, 128), 128)
                        dp[row0 : row0 + rows, w] = part[:, q * 128 : q * 128 + 128].astype(BF16)

            for t in range(2):
                mine = z_own + t == rb if on_z else lax.rem(g_own, 4) == rb

                @pl.when(mine)
                def _():
                    w = cols((z_own + t) * 8 + g_own if on_z else g_own * 4 + z_own + t, 128)
                    dp[row0 : row0 + rows, w] = (
                        f32(dp[row0 : row0 + rows, w]) + f32(S["hg"][row0 : row0 + rows, t * 128 : t * 128 + 128])
                    ).astype(BF16)

            ks.append(
                [send(dp.at[dhalf(1 - core), dcols(rb, h)], B["cr"].at[:, dcols(rb, h)], cp) for h in range(2)]
            )
            yield "back"
            if i == 1:
                finish(0)
                a = send(dwin(0, order[0]), rel.at[0], big_dev[0])
                b = send(dwin(1, order[0]), rel.at[1], big_dev[1])
            if i == 2:
                finish(1)
                c1 = send(dwin(1, order[1]), rl.at[1], big_dev[0])
            if i == 3:
                finish(2)
                d0 = send(dwin(0, order[2]), rr.at[0], big_dev[1])
        total = yield from rs_tail(dwin, bufs["c5"], big, big_dev, yl, lp, a, b, c1, d0, lambda: finish(3))
        B["E5"][...] = total.astype(BF16)
        total = yield from rs_far(
            lambda h, r: B["E5"].at[pl.ds(pl.multiple_of(h * r4, r4), r4), cols(r, 128)], B["e5"], yh, small, far_small
        )
        dt = B["dt"]
        dt[quarter(core, yh), cols(z, 128)] = total.astype(BF16)
        yield from ag_far(lambda h, r: dt.at[quarter(core, h), cols(r, 128)], yh, z, far_z)
        k = send(dt.at[half(core)], dt.at[half(core)], cp)
        yield
        k.wait_recv()
        keep = net.copy(dt.at[pl.ds(m * r16, r16)], B["own"])
        for n, w in TILES:
            part = dot_t(dt[...], S["td"][n : n + w, :])
            for j in range(8):
                B["G7"][j, :, n : n + w] = part[j * r8 : (j + 1) * r8].astype(BF16)
        more = rs_far(lambda h, r: B["G7"].at[h * 4 + r], B["c7"], yl, x, far_g)
        next(more)

        def gather_rows(out, left, right):
            first = once(out)
            for n, w in TILES:
                part = contract_first(left[:, n : n + w], right)
                if first:
                    outs[out][n : n + w, :] = part
                else:
                    outs[out][n : n + w, :] += part

        gather_rows(3, hid[...].reshape(rows, FL), dt[...])
        yield
        total = yield from more
        gh, dgu = B["gh"], B["dgu"]
        gh[g] = total.astype(BF16)
        yield from ag_far(lambda h, r: gh.at[h * 4 + r], yl, x, far_g)
        for i in range(2):
            dgu[i] = (f32(gh[...]) * f32(ab[i])).astype(BF16).reshape(rows, FL)
        part = dot(dgu[0], S["tg"][...]) + dot(dgu[1], S["tu"][...])
        X9 = B["X9"]
        for i in range(16):
            X9[i % 2, i // 8, i // 2 % 4] = part[i * r16 : (i + 1) * r16].astype(BF16)
        k = send(X9.at[1 - core], B["X9r"], cp)
        gather_rows(1, dgu[0], B["tok"][...])
        yield
        k.wait_recv()
        acc(X9.at[core], B["X9r"])
        more = rs_far(lambda h, r: X9.at[core, h, r], B["c9"], yh, z, far_z)
        next(more)
        gather_rows(2, dgu[1], B["tok"][...])
        yield
        total = yield from more
        keep.wait()
        outs[0][sum(FINAL[:c]) : sum(FINAL[: c + 1]), :] = (f32(B["own"][...]) + total).astype(BF16)

    gens = {"c": gather_cot(), "h": head_hidden()} | {str(c): chunk(c) for c in range(len(ROWS))}

    def step(gen):
        return next(gen, "end")

    for c in range(len(ROWS)):
        step(gens[str(c)])
    pl.semaphore_wait(barrier, len(near))
    for name in "".join(ORDER):
        step(gens[name])
    for gen in gens.values():
        while step(gen) != "end":
            pass
    for copy in net.sent:
        copy.wait_send()


def body(tokens, trunk_gate, trunk_up, trunk_down, head_gate, head_up, head_down, head_grads):
    names, shapes = layout()
    grad_x, grad_gate, grad_up, grad_down = pl.pallas_call(
        functools.partial(kernel, names),
        out_shape=[
            pltpu.VMEM((sum(FINAL), CW), BF16),
            pltpu.VMEM((FL, CW), F32),
            pltpu.VMEM((FL, CW), F32),
            pltpu.VMEM((FL, CW), F32),
        ],
        in_specs=[pl.BlockSpec(memory_space=pl.ANY)] * 8,
        out_specs=[pl.BlockSpec(memory_space=pltpu.VMEM)] * 4,
        scratch_shapes=[
            *shapes,
            pltpu.SemaphoreType.DMA((N_SEM,)),
            pltpu.SemaphoreType.DMA((N_SEM,)),
            pltpu.SemaphoreType.DMA((220,)),
        ],
        compiler_params=pltpu.CompilerParams(
            collective_id=0, has_side_effects=True, vmem_limit_bytes=62500000
        ),
    )(
        tokens,
        trunk_gate.T,
        trunk_up.T,
        trunk_down,
        head_gate[0].T,
        head_up[0].T,
        head_down[0],
        head_grads[0],
    )
    return grad_x, grad_gate.T, grad_up.T, grad_down


def solution(mesh):
    return jax.shard_map(
        body,
        mesh=mesh,
        in_specs=(
            P(None, "group"),
            P("group", "mp"),
            P("group", "mp"),
            P("mp", "group"),
            P("group", None, "mp"),
            P("group", None, "mp"),
            P("group", "mp", None),
            P("group", None, "mp"),
        ),
        out_specs=(P("mp", "group"), P("group", "mp"), P("group", "mp"), P("mp", "group")),
        check_vma=False,
    )
```
